256 devices in a mesh: ep: 32 (over y, z_hi, core), dp: 8 (over z_lo, x).
Axes of the slice: x: 4, y: 4, z: 8 (z_hi: 4, z_lo: 2; z = z_hi * 2 + z_lo), core: 2. Of those that a mesh axis runs over, the one named last changes fastest.
Arguments:
- gradients: float32 [8, 4096, 7168], P('dp', 'ep'), may hold values from -18 to 18
- master_rows: float32 [32, 192, 7168], P('ep', 'dp'), may hold values from -0.24 to 0.24
- first_moment: float32 [32, 192, 7168], P('ep', 'dp'), may hold values from -2 to 2
- second_moment: float32 [32, 192, 7168], P('ep', 'dp'), may hold values from 0.1 to 1
- shard_rows: int32 [32, 8], replicated, may hold values from 1 to 24, as said below
- move_partner: int32 [32], replicated, may hold values from 0 to 31, as said below
Outputs:
- new_master: float32 [32, 192, 7168], P('ep', 'dp')
- new_first: float32 [32, 192, 7168], P('ep', 'dp')
- new_second: float32 [32, 192, 7168], P('ep', 'dp')
- placed_params: bfloat16 [4096, 7168], P('ep')
The draws below stay inside these ranges and needn't reach their ends.
Inputs may be any that keep to these rules, and one draw needn't show every extreme that they name: `shard_rows`: in each row the shards own consecutive runs of the 128 flat rows in order, each at least one row, summing to 128; the largest of each row is exactly 24. move_partner[i] is i or i with one binary digit flipped; that digit is the same for every i that moves; move_partner[move_partner[i]] == i.
All inputs are finite; a program needn't handle non-finite values.
Results may differ from the reference program's by a relative error of at most 0.014.
Values may be sent and summed in bfloat16 or wider, within the bound.
No kernel may reach another device: no remote copies, remote signals or barrier semaphores. Data moves between devices by JAX's collectives and lax.ppermute only.
A program may use at most 128 MiB of HBM per device.

```python
import math
import jax
import jax.numpy as jnp
from jax import lax

D = 7168
FLAT = 128
CAP = 24
N_EP = 32
N_DP = 8


def draw_move_partner(key, part):
    indices = jnp.arange(N_EP, dtype=jnp.int32)
    bit_count = int(N_EP).bit_length() - 1
    key_bit, key_coin = jax.random.split(key)
    chosen = jax.random.randint(key_bit, (), 0, bit_count, dtype=jnp.int32)
    other_side = jnp.bitwise_xor(indices, jnp.left_shift(jnp.int32(1), chosen))
    lower = jnp.minimum(indices, other_side)
    coins = jax.random.randint(key_coin, (N_EP,), 0, 2, dtype=jnp.int32)
    partner = jnp.where(coins[lower] == 1, other_side, indices)
    return partner.astype(jnp.int32)


def shard_row_counts(row_key):
    key_place, key_spread = jax.random.split(row_key)
    indices = jnp.arange(N_DP, dtype=jnp.int32)
    largest = jax.random.randint(key_place, (), 0, N_DP, dtype=jnp.int32)
    counts = jnp.where(indices == largest, CAP, 1).astype(jnp.int32)
    room = jnp.where(indices == largest, 0, CAP - 1).astype(jnp.int32)
    extra = FLAT - CAP - (N_DP - 1)

    def spread_one(step, carry):
        current, left = carry
        scores = jax.random.randint(jax.random.fold_in(key_spread, step), (N_DP,), 0, 1024, dtype=jnp.int32) * N_DP + indices
        scores = jnp.where(left > 0, scores, -1)
        picked = jnp.argmax(scores).astype(jnp.int32)
        hit = (indices == picked).astype(jnp.int32)
        return (current + hit, left - hit)
    counts, room = lax.fori_loop(0, extra, spread_one, (counts, room))
    return counts.astype(jnp.int32)


def draw_shard_rows(key, part):
    row_keys = jax.random.split(jax.random.fold_in(key, 17), N_EP)
    return jax.vmap(shard_row_counts)(row_keys).astype(jnp.int32)


def level_of(key, dims, cuts, smallest, top_value):
    loudness, own = 1.0, jax.random.fold_in(key, 6)
    for dim, shards_of in cuts:
        steps = jnp.exp(jax.random.uniform(jax.random.fold_in(own, dim), (shards_of,), jnp.float32, smallest / len(cuts), top_value / len(cuts)))
        loudness = loudness * jnp.repeat(steps, dims[dim] // shards_of).reshape([-1 if axis == dim else 1 for axis in range(len(dims))])
    return loudness


def centred(own_key, extent, scale, limit, cuts=(), held_as=jnp.bfloat16):
    result = jax.random.normal(own_key, extent, jnp.float32) * scale
    if len(cuts) > 0:
        result = level_of(own_key, extent, cuts, -0.22, 0.18) * result
    return jnp.clip(result, min=-limit, max=limit).astype(held_as)


def setup_inputs(seed: int = 0) -> dict:
    key_of = jax.random.split(jax.random.key(seed), 7)
    gradients = centred(key_of[0], (N_DP, N_EP * FLAT, D), 3.0, 18.0, ((0, 8), (1, 32)), jnp.float32)
    master_rows = centred(key_of[1], (N_EP, N_DP * CAP, D), 0.04, 0.24, ((0, 32), (1, 8)), jnp.float32)
    first_moment = centred(key_of[2], (N_EP, N_DP * CAP, D), 0.3, 2.0, ((0, 32), (1, 8)), jnp.float32)
    second_moment = jnp.clip(jnp.exp(math.log(1.0) - 2.3025851 * jax.random.uniform(key_of[3], (N_EP, N_DP * CAP, D), jnp.float32) ** level_of(key_of[3], (N_EP, N_DP * CAP, D), ((0, 32), (1, 8)), -0.2, 0.2)), 0.1, 1.0)
    shard_rows = draw_shard_rows(jax.random.fold_in(key_of[6], 71), 0)
    move_partner = draw_move_partner(jax.random.fold_in(key_of[6], 71), 0)
    return {"gradients": gradients, "master_rows": master_rows, "first_moment": first_moment, "second_moment": second_moment, "shard_rows": shard_rows, "move_partner": move_partner}


beta_one = 0.9
beta_two = 0.95
learn_rate = 0.02
weight_decay = 0.1
epsilon = 1e-08
correct_one = 1.0 - 0.9 ** 10
correct_two = 1.0 - 0.95 ** 10

def adam_step(grad_rows, weights, first, second, live):
    first_new = beta_one * first + (1.0 - beta_one) * grad_rows
    second_new = beta_two * second + (1.0 - beta_two) * grad_rows * grad_rows
    ratio = first_new / correct_one / (jnp.sqrt(second_new / correct_two) + epsilon)
    updated = weights - learn_rate * (ratio + weight_decay * weights)
    return (jnp.where(live, updated, 0.0), jnp.where(live, first_new, 0.0), jnp.where(live, second_new, 0.0))

def one_group(grad_group, master_group, first_group, second_group, counts):
    starts = (jnp.cumsum(counts) - counts).astype(jnp.int32)
    slots = jnp.arange(N_DP * CAP, dtype=jnp.int32)
    owners = slots // CAP
    within = slots % CAP
    live = within < counts[owners]
    source = jnp.minimum(starts[owners] + within, FLAT - 1).astype(jnp.int32)
    grad_pad = jnp.where(live[:, None], grad_group[source, :], 0.0)
    return adam_step(grad_pad, master_group, first_group, second_group, live[:, None])

def place_group(master_group, counts):
    starts = (jnp.cumsum(counts) - counts).astype(jnp.int32)
    flat_rows = jnp.arange(FLAT, dtype=jnp.int32)
    owner_flat = lax.optimization_barrier(jnp.sum((flat_rows[:, None] >= starts[None, 1:]).astype(jnp.int32), axis=1)).astype(jnp.int32)
    position = (owner_flat * CAP + flat_rows - starts[owner_flat]).astype(jnp.int32)
    return master_group[position, :]

def reference(gradients, master_rows, first_moment, second_moment, shard_rows, move_partner):
    counts = shard_rows.astype(jnp.int32)
    grad_mean = (lax.optimization_barrier(jnp.sum(gradients, axis=0)) / N_DP).reshape(N_EP, FLAT, D)
    updated, first_new, second_new = jax.vmap(one_group)(grad_mean, master_rows, first_moment, second_moment, counts)
    new_master = updated[move_partner]
    new_first = first_new[move_partner]
    new_second = second_new[move_partner]
    moved_counts = counts[move_partner]
    placed = jax.vmap(place_group)(new_master, moved_counts).astype(jnp.bfloat16).reshape(N_EP * FLAT, D)
    return (new_master, new_first, new_second, placed)
```

```python
import jax
import jax.numpy as jnp
from jax import lax
from jax.sharding import PartitionSpec as P

beta_one = 0.9
beta_two = 0.95
learn_rate = 0.02
weight_decay = 0.1
epsilon = 1e-08
correct_one = 1.0 - 0.9**10
correct_two = 1.0 - 0.95**10


def swapped(array, axis, apart):
    return lax.ppermute(array, axis, [(i, i ^ 1 << apart) for i in range(lax.axis_size(axis))])


def adam_step(grad_rows, weights, first, second, live):
    first_new = beta_one * first + (1.0 - beta_one) * grad_rows
    second_new = beta_two * second + (1.0 - beta_two) * grad_rows * grad_rows
    ratio = first_new / correct_one / (jnp.sqrt(second_new / correct_two) + epsilon)
    updated = weights - learn_rate * (ratio + weight_decay * weights)
    return (
        jnp.where(live, updated, 0.0),
        jnp.where(live, first_new, 0.0),
        jnp.where(live, second_new, 0.0),
    )


def starts_of(counts):
    shards = jnp.arange(counts.shape[0], dtype=jnp.int32)
    earlier = shards[:, None] < shards[None, :]
    return jnp.sum(jnp.where(earlier, counts[:, None], 0), axis=0)


def slot_of_row(counts, capacity, slot_count, flat_count):
    starts = starts_of(counts)
    slots = jnp.arange(slot_count, dtype=jnp.int32)
    owners = slots // capacity
    within = slots % capacity
    shards = jnp.arange(counts.shape[0], dtype=jnp.int32)
    mine = owners[:, None] == shards[None, :]
    start = jnp.sum(jnp.where(mine, starts[None, :], 0), axis=1)
    count = jnp.sum(jnp.where(mine, counts[None, :], 0), axis=1)
    source = jnp.where(within < count, start + within, -1)
    return source[:, None] == jnp.arange(flat_count, dtype=jnp.int32)[None, :]


def body(gradients, master_rows, first_moment, second_moment, shard_rows, move_partner):
    groups = lax.axis_size("dp")
    capacity = master_rows.shape[1]
    flat_count = gradients.shape[1]
    dp_index = lax.axis_index("dp")
    ep_index = lax.axis_index("ep")
    partner = move_partner[ep_index]
    counts = shard_rows[ep_index]
    moved_counts = shard_rows[partner]
    live = (jnp.arange(capacity, dtype=jnp.int32) < counts[dp_index])[:, None]
    moves = partner != ep_index
    flipped = jnp.max(jnp.bitwise_xor(move_partner, jnp.arange(move_partner.shape[0], dtype=jnp.int32)))
    bits = lax.axis_size("ep").bit_length() - 1
    which_bit = sum((flipped >= 1 << b).astype(jnp.int32) for b in range(1, bits))

    pack = slot_of_row(counts, capacity, groups * capacity, flat_count).astype(jnp.bfloat16)
    place = slot_of_row(moved_counts, capacity, groups * capacity, flat_count).astype(jnp.bfloat16)

    def step(apart, operands):
        gradients, master_rows, first_moment, second_moment, pack, place, live, moves = operands
        packed = lax.dot_general(
            pack,
            gradients[0].astype(jnp.bfloat16),
            (((1,), (0,)), ((), ())),
            preferred_element_type=jnp.float32,
        ).astype(jnp.bfloat16)
        summed = lax.psum_scatter(packed, "dp", scatter_dimension=0, tiled=True).astype(jnp.float32)
        updated, first_new, second_new = adam_step(
            summed / groups, master_rows[0], first_moment[0], second_moment[0], live
        )

        def moved(values):
            arrived = swapped(values.astype(jnp.bfloat16), "ep", apart).astype(values.dtype)
            return jnp.where(moves, arrived, values)

        new_master = moved(updated)
        whole = lax.all_gather(new_master.astype(jnp.bfloat16), "dp", axis=0, tiled=True)
        new_first = moved(first_new)
        new_second = moved(second_new)
        placed = lax.dot_general(
            place, whole, (((0,), (0,)), ((), ())), preferred_element_type=jnp.float32
        ).astype(jnp.bfloat16)
        return new_master[None], new_first[None], new_second[None], placed

    operands = (gradients, master_rows, first_moment, second_moment, pack, place, live, moves)
    return lax.switch(which_bit, [lambda o, b=b: step(b, o) for b in range(bits)], operands)


def solution(mesh):
    placed = (
        P("dp", "ep", None),
        P("ep", "dp", None),
        P("ep", "dp", None),
        P("ep", "dp", None),
        P(),
        P(),
    )
    return jax.shard_map(
        body,
        mesh=mesh,
        in_specs=placed,
        out_specs=(P("ep", "dp", None), P("ep", "dp", None), P("ep", "dp", None), P("ep", None)),
        check_vma=False,
    )
```

```python
import jax
import jax.numpy as jnp
from jax import lax
from jax.experimental import pallas as pl
from jax.experimental.pallas import tpu as pltpu
from jax.sharding import PartitionSpec as P

beta_one = 0.9
beta_two = 0.95
learn_rate = 0.02
weight_decay = 0.1
epsilon = 1e-08
correct_one = 1.0 - 0.9**10
correct_two = 1.0 - 0.95**10

orders = ((4, 1, 3), (1, 3, 4), (3, 4, 1))


def flipped_by(array, axis, mask):
    return lax.ppermute(array, axis, [(i, i ^ mask) for i in range(lax.axis_size(axis))])


def adam_step(grad_rows, weights, first, second, live):
    first_new = beta_one * first + (1.0 - beta_one) * grad_rows
    second_new = beta_two * second + (1.0 - beta_two) * grad_rows * grad_rows
    ratio = first_new / correct_one / (jnp.sqrt(second_new / correct_two) + epsilon)
    updated = weights - learn_rate * (ratio + weight_decay * weights)
    return (
        jnp.where(live, updated, 0.0),
        jnp.where(live, first_new, 0.0),
        jnp.where(live, second_new, 0.0),
    )


def starts_of(counts):
    shards = jnp.arange(counts.shape[0], dtype=jnp.int32)
    earlier = shards[:, None] < shards[None, :]
    return jnp.sum(jnp.where(earlier, counts[:, None], 0), axis=0)


def row_of_slot(counts, dp_index, order, capacity):
    shards = jnp.arange(8, dtype=jnp.int32)
    slots = jnp.arange(8 * capacity, dtype=jnp.int32)
    place = slots // capacity
    within = slots % capacity
    relative = (place >> 2 & 1) * order[0] ^ (place >> 1 & 1) * order[1] ^ (place & 1) * order[2]
    mine = (relative ^ dp_index)[:, None] == shards[None, :]
    start = jnp.sum(jnp.where(mine, starts_of(counts)[None, :], 0), axis=1)
    count = jnp.sum(jnp.where(mine, counts[None, :], 0), axis=1)
    return jnp.where(within < count, start + within, -1)


def slot_of_row(counts, dp_index, order, capacity, flat_count):
    rows = row_of_slot(counts, dp_index, order, capacity)
    flat = jnp.arange(flat_count, dtype=jnp.int32)
    slots = jnp.arange(8 * capacity, dtype=jnp.int32)
    return jnp.sum(jnp.where(rows[None, :] == flat[:, None], slots[None, :], 0), axis=1)


def place_kernel(groups_cols, capacity, slots_ref, *refs):
    out_ref = refs[-1]
    sizes = (capacity, capacity, 2 * capacity, 4 * capacity)
    begin = 0
    for g, cols in enumerate(groups_cols):
        slot = slots_ref[:, g : g + 1]
        total = None
        at = 0
        for size, ref in zip(sizes, refs[4 * g : 4 * g + 4]):
            hot = slot == at + lax.broadcasted_iota(jnp.int32, (slot.shape[0], size), 1)
            part = jnp.dot(
                jnp.where(hot, 1.0, 0.0).astype(jnp.bfloat16), ref[...], preferred_element_type=jnp.float32
            )
            total = part if total is None else total + part
            at += size
        out_ref[:, begin : begin + cols] = total.astype(jnp.bfloat16)
        begin += cols


def body(gradients, master_rows, first_moment, second_moment, shard_rows, move_partner):
    capacity = master_rows.shape[1]
    flat_count, width = gradients.shape[1:]
    lanes = width // 128
    cuts = [128 * (lanes * i // 3) for i in range(4)]
    groups_cols = [b - a for a, b in zip(cuts, cuts[1:])]
    dp_index = lax.axis_index("dp")
    ep_index = lax.axis_index("ep")
    ep_all = jnp.arange(move_partner.shape[0], dtype=jnp.int32)
    counts = jnp.sum(jnp.where((ep_all == ep_index)[:, None], shard_rows, 0), axis=0)

    flat = jnp.arange(flat_count, dtype=jnp.int32)
    sums = []
    half = 4 * capacity
    for g, order in enumerate(orders):
        rows = row_of_slot(counts, dp_index, order, capacity)
        pack = (rows[:, None] == flat[None, :]).astype(jnp.bfloat16)
        columns = gradients[0, :, cuts[g] : cuts[g + 1]].astype(jnp.bfloat16)
        send = jnp.dot(pack[half:], columns, preferred_element_type=jnp.float32).astype(jnp.bfloat16)
        kept = jnp.dot(pack[:half], columns, preferred_element_type=jnp.float32).astype(jnp.bfloat16)
        sums.append((send, kept))
    rest = half
    for step in range(3):
        arrived = [flipped_by(send, "dp", orders[g][step]) for g, (send, _) in enumerate(sums)]
        rest //= 2
        for g in range(3):
            kept = sums[g][1].astype(jnp.float32) + arrived[g].astype(jnp.float32)
            sums[g] = (kept[rest:].astype(jnp.bfloat16), kept[:rest]) if step < 2 else (None, kept)
    grad_own = jnp.concatenate([kept for _, kept in sums], axis=1) / 8

    partner = jnp.sum(jnp.where(ep_all == ep_index, move_partner, 0))
    moved_counts = jnp.sum(jnp.where((ep_all == partner)[:, None], shard_rows, 0), axis=0)
    own_count = jnp.sum(jnp.where(jnp.arange(8, dtype=jnp.int32) == dp_index, counts, 0))
    live = (jnp.arange(capacity, dtype=jnp.int32) < own_count)[:, None]
    moves = partner != ep_index
    flips = jnp.bitwise_xor(move_partner, ep_all)
    bits = move_partner.shape[0].bit_length() - 1
    which_bit = jnp.max(sum((flips >= 1 << b).astype(jnp.int32) for b in range(1, bits)))
    slots = jnp.stack(
        [slot_of_row(moved_counts, dp_index, order, capacity, flat_count) for order in orders], axis=1
    )

    def finish(apart, operands):
        grad_own, master_rows, first_moment, second_moment, slots, live, moves = operands
        updated, first_new, second_new = adam_step(
            grad_own, master_rows[0], first_moment[0], second_moment[0], live
        )

        def moved(values):
            arrived = flipped_by(values.astype(jnp.bfloat16), "ep", 1 << apart).astype(values.dtype)
            return jnp.where(moves, arrived, values)

        new_master = moved(updated)
        narrow = new_master.astype(jnp.bfloat16)
        pieces = [[narrow[:, cuts[g] : cuts[g + 1]]] for g in range(3)]
        for step in range(3):
            sent = [p[0] if step == 0 else jnp.concatenate(p, axis=0) for p in pieces]
            for g in range(3):
                pieces[g].append(flipped_by(sent[g], "dp", orders[g][2 - step]))
        new_first = moved(first_new)
        new_second = moved(second_new)
        placed = pl.pallas_call(
            lambda *refs: place_kernel(groups_cols, capacity, *refs),
            out_shape=jax.ShapeDtypeStruct((flat_count, width), jnp.bfloat16),
            compiler_params=pltpu.CompilerParams(vmem_limit_bytes=48 * 1024 * 1024),
            name="place",
        )(slots, *[piece for group in pieces for piece in group])
        return new_master[None], new_first[None], new_second[None], placed

    operands = (grad_own, master_rows, first_moment, second_moment, slots, live, moves)
    return lax.switch(which_bit, [lambda o, b=b: finish(b, o) for b in range(bits)], operands)


def solution(mesh):
    placed = (
        P("dp", "ep", None),
        P("ep", "dp", None),
        P("ep", "dp", None),
        P("ep", "dp", None),
        P(),
        P(),
    )
    return jax.shard_map(
        body,
        mesh=mesh,
        in_specs=placed,
        out_specs=(P("ep", "dp", None), P("ep", "dp", None), P("ep", "dp", None), P("ep", None)),
        check_vma=False,
    )
```

```python
import jax
import jax.numpy as jnp
from jax import lax
from jax.experimental import pallas as pl
from jax.experimental.pallas import tpu as pltpu
from jax.sharding import PartitionSpec as P

beta_one = 0.9
beta_two = 0.95
learn_rate = 0.02
weight_decay = 0.1
epsilon = 1e-08
correct_one = 1.0 - 0.9**10
correct_two = 1.0 - 0.95**10

orders = ((4, 1, 3), (1, 3, 4), (3, 4, 1))
vmem_bytes = 48 * 1024 * 1024


def flipped_by(array, axis, mask):
    return lax.ppermute(array, axis, [(i, i ^ mask) for i in range(lax.axis_size(axis))])


def adam_step(grad_rows, weights, first, second, live):
    first_new = beta_one * first + (1.0 - beta_one) * grad_rows
    second_new = beta_two * second + (1.0 - beta_two) * grad_rows * grad_rows
    ratio = first_new / correct_one / (jnp.sqrt(second_new / correct_two) + epsilon)
    updated = weights - learn_rate * (ratio + weight_decay * weights)
    return (
        jnp.where(live, updated, 0.0),
        jnp.where(live, first_new, 0.0),
        jnp.where(live, second_new, 0.0),
    )


def slots_to_rows(rows_ref, ep_index, dp_index, order, capacity, flat_count):
    shards = rows_ref.shape[0]
    counts = [rows_ref[k, ep_index] for k in range(shards)]
    starts = [jnp.int32(0)]
    for k in range(shards - 1):
        starts.append(starts[-1] + counts[k])
    slot = lax.broadcasted_iota(jnp.int32, (capacity, flat_count), 0)
    flat = lax.broadcasted_iota(jnp.int32, (capacity, flat_count), 1)
    blocks = []
    for p in range(shards):
        k = dp_index ^ ((p >> 2 & 1) * order[0] ^ (p >> 1 & 1) * order[1] ^ (p & 1) * order[2])
        start, count = starts[0], counts[0]
        for j in range(1, shards):
            start = jnp.where(k == j, starts[j], start)
            count = jnp.where(k == j, counts[j], count)
        blocks.append(jnp.where((flat - slot == start) & (slot < count), 1.0, 0.0))
    return jnp.concatenate(blocks, axis=0)


smem_spec = pl.BlockSpec(memory_space=pltpu.SMEM)
vmem_spec = pl.BlockSpec(memory_space=pltpu.VMEM)
params = pltpu.CompilerParams(vmem_limit_bytes=vmem_bytes)


def pack_kernel(cuts, capacity, place_ref, rows_ref, grad_ref, *refs):
    outs, (columns_ref, sems) = refs[:6], refs[6:]
    flat_count = grad_ref.shape[1]
    copies = []
    for g in range(3):
        part = pl.ds(cuts[g], cuts[g + 1] - cuts[g])
        copies.append(pltpu.make_async_copy(grad_ref.at[0, :, part], columns_ref.at[:, part], sems.at[g]))
        copies[-1].start()
    half = 4 * capacity
    for g in range(3):
        hot = slots_to_rows(rows_ref, place_ref[0], place_ref[1], orders[g], capacity, flat_count)
        hot = hot.astype(jnp.bfloat16)
        copies[g].wait()
        columns = columns_ref[:, cuts[g] : cuts[g + 1]].astype(jnp.bfloat16)
        packed = jnp.dot(hot, columns, preferred_element_type=jnp.float32).astype(jnp.bfloat16)
        outs[g][...] = packed[half:]
        outs[3 + g][...] = packed[:half]


def pack(where, rows_by_shard, gradients, cuts, capacity):
    flat_count, width = gradients.shape[1:]
    shapes = [
        jax.ShapeDtypeStruct((4 * capacity, cuts[g + 1] - cuts[g]), jnp.bfloat16) for g in (0, 1, 2, 0, 1, 2)
    ]
    return pl.pallas_call(
        lambda *refs: pack_kernel(cuts, capacity, *refs),
        in_specs=[smem_spec, smem_spec, pl.BlockSpec(memory_space=pltpu.HBM)],
        out_specs=[vmem_spec] * 6,
        out_shape=shapes,
        scratch_shapes=[pltpu.VMEM((flat_count, width), jnp.float32), pltpu.SemaphoreType.DMA((3,))],
        compiler_params=params,
        name="pack",
    )(where, rows_by_shard, gradients)


def sum_kernel(*refs):
    kept, arrived, outs = refs[:3], refs[3:6], refs[6:]
    rest = kept[0].shape[0] // 2
    for g in range(3):
        outs[g][...] = (
            kept[g][rest:].astype(jnp.float32) + arrived[g][rest:].astype(jnp.float32)
        ).astype(jnp.bfloat16)
        outs[3 + g][...] = kept[g][:rest].astype(jnp.float32) + arrived[g][:rest].astype(jnp.float32)


def summed(kept, arrived):
    shapes = [
        jax.ShapeDtypeStruct((k.shape[0] // 2, k.shape[1]), dtype)
        for dtype in (jnp.bfloat16, jnp.float32)
        for k in kept
    ]
    outs = pl.pallas_call(
        sum_kernel,
        in_specs=[vmem_spec] * 6,
        out_specs=[vmem_spec] * 6,
        out_shape=shapes,
        compiler_params=params,
        name="sums",
    )(*kept, *arrived)
    return outs[:3], outs[3:]


def place_kernel(cuts, capacity, place_ref, rows_ref, *refs):
    here, arrived, out_ref = refs[:3], refs[3:6], refs[6]
    half = 4 * capacity
    for g in range(3):
        hot = slots_to_rows(rows_ref, place_ref[2], place_ref[1], orders[g], capacity, out_ref.shape[0])
        hot = hot.T.astype(jnp.bfloat16)
        total = jnp.dot(hot[:, :half], here[g][...], preferred_element_type=jnp.float32)
        total += jnp.dot(hot[:, half:], arrived[g][...], preferred_element_type=jnp.float32)
        out_ref[:, cuts[g] : cuts[g + 1]] = total.astype(jnp.bfloat16)


def place(where, rows_by_shard, here, arrived, cuts, capacity, flat_count):
    return pl.pallas_call(
        lambda *refs: place_kernel(cuts, capacity, *refs),
        in_specs=[smem_spec, smem_spec] + [vmem_spec] * 6,
        out_shape=jax.ShapeDtypeStruct((flat_count, cuts[-1]), jnp.bfloat16),
        compiler_params=params,
        name="place",
    )(where, rows_by_shard, *here, *arrived)


def body(gradients, master_rows, first_moment, second_moment, shard_rows, move_partner):
    capacity = master_rows.shape[1]
    flat_count, width = gradients.shape[1:]
    lanes = width // 128
    cuts = [128 * (lanes * i // 3) for i in range(4)]
    dp_index = lax.axis_index("dp")
    ep_index = lax.axis_index("ep")
    ep_all = jnp.arange(move_partner.shape[0], dtype=jnp.int32)
    where = jnp.stack([ep_index, dp_index]).astype(jnp.int32)

    rows_by_shard = shard_rows.T
    packed = pack(where, rows_by_shard, gradients, cuts, capacity)
    sent, kept = packed[:3], packed[3:]
    for step in range(3):
        arrived = [flipped_by(sent[g], "dp", orders[g][step]) for g in range(3)]
        if step < 2:
            sent, kept = summed(kept, arrived)
    grad_own = jnp.concatenate([k + a.astype(jnp.float32) for k, a in zip(kept, arrived)], axis=1) / 8

    partner = jnp.sum(jnp.where(ep_all == ep_index, move_partner, 0))
    own_counts = jnp.sum(jnp.where((ep_all == ep_index)[:, None], shard_rows, 0), axis=0)
    own_count = jnp.sum(jnp.where(jnp.arange(8, dtype=jnp.int32) == dp_index, own_counts, 0))
    live = (jnp.arange(capacity, dtype=jnp.int32) < own_count)[:, None]
    moves = partner != ep_index
    flips = jnp.bitwise_xor(move_partner, ep_all)
    bits = move_partner.shape[0].bit_length() - 1
    which_bit = jnp.max(sum((flips >= 1 << b).astype(jnp.int32) for b in range(1, bits)))

    updated, first_new, second_new = adam_step(
        grad_own, master_rows[0], first_moment[0], second_moment[0], live
    )

    def relocated(apart, arrays):
        return [flipped_by(a, "ep", 1 << apart) for a in arrays]

    sent_master = updated.astype(jnp.bfloat16)
    (there,) = lax.switch(
        which_bit, [lambda o, b=b: relocated(b, o) for b in range(bits)], [sent_master]
    )
    narrow = jnp.where(moves, there, sent_master)
    here = [narrow[:, cuts[g] : cuts[g + 1]] for g in range(3)]
    for step in range(2):
        arrived = [flipped_by(here[g], "dp", orders[g][2 - step]) for g in range(3)]
        arrived = lax.optimization_barrier(arrived)
        here = [jnp.concatenate(pair, axis=0) for pair in zip(here, arrived)]

    def last(apart, operands):
        here, moments = operands
        arrived = [flipped_by(here[g], "dp", orders[g][0]) for g in range(3)]
        return arrived, relocated(apart, moments)

    moments = [first_new.astype(jnp.bfloat16), second_new.astype(jnp.bfloat16)]
    arrived, moments = lax.switch(
        which_bit, [lambda o, b=b: last(b, o) for b in range(bits)], (here, moments)
    )
    placed = place(
        jnp.stack([ep_index, dp_index, partner]).astype(jnp.int32),
        rows_by_shard,
        here,
        arrived,
        cuts,
        capacity,
        flat_count,
    )
    new_master, new_first, new_second = [
        jnp.where(moves, arrived.astype(jnp.float32), own)[None]
        for arrived, own in ((there, updated), (moments[0], first_new), (moments[1], second_new))
    ]
    return new_master, new_first, new_second, placed


def solution(mesh):
    placed = (
        P("dp", "ep", None),
        P("ep", "dp", None),
        P("ep", "dp", None),
        P("ep", "dp", None),
        P(),
        P(),
    )
    return jax.shard_map(
        body,
        mesh=mesh,
        in_specs=placed,
        out_specs=(P("ep", "dp", None), P("ep", "dp", None), P("ep", "dp", None), P("ep", None)),
        check_vma=False,
    )
```

```python
import jax
import jax.numpy as jnp
from jax import lax
from jax.experimental import pallas as pl
from jax.experimental.pallas import tpu as pltpu
from jax.sharding import PartitionSpec as P

beta_one = 0.9
beta_two = 0.95
learn_rate = 0.02
weight_decay = 0.1
epsilon = 1e-08
correct_one = 1.0 - 0.9**10
correct_two = 1.0 - 0.95**10

orders = ((4, 1, 3), (1, 3, 4), (3, 4, 1))
vmem_bytes = 48 * 1024 * 1024


def flipped_by(array, axis, mask):
    return lax.ppermute(array, axis, [(i, i ^ mask) for i in range(lax.axis_size(axis))])


def adam_step(grad_rows, weights, first, second, live):
    first_new = beta_one * first + (1.0 - beta_one) * grad_rows
    second_new = beta_two * second + (1.0 - beta_two) * grad_rows * grad_rows
    ratio = first_new / correct_one / (jnp.sqrt(second_new / correct_two) + epsilon)
    updated = weights - learn_rate * (ratio + weight_decay * weights)
    return (
        jnp.where(live, updated, 0.0),
        jnp.where(live, first_new, 0.0),
        jnp.where(live, second_new, 0.0),
    )


def slots_to_rows(rows_ref, ep_index, dp_index, order, capacity, flat_count):
    shards = rows_ref.shape[0]
    counts = [rows_ref[k, ep_index] for k in range(shards)]
    starts = [jnp.int32(0)]
    for k in range(shards - 1):
        starts.append(starts[-1] + counts[k])
    slot = lax.broadcasted_iota(jnp.int32, (capacity, flat_count), 0)
    flat = lax.broadcasted_iota(jnp.int32, (capacity, flat_count), 1)
    blocks = []
    for p in range(shards):
        k = dp_index ^ ((p >> 2 & 1) * order[0] ^ (p >> 1 & 1) * order[1] ^ (p & 1) * order[2])
        start, count = starts[0], counts[0]
        for j in range(1, shards):
            start = jnp.where(k == j, starts[j], start)
            count = jnp.where(k == j, counts[j], count)
        blocks.append(jnp.where((flat - slot == start) & (slot < count), 1.0, 0.0))
    return jnp.concatenate(blocks, axis=0)


smem_spec = pl.BlockSpec(memory_space=pltpu.SMEM)
vmem_spec = pl.BlockSpec(memory_space=pltpu.VMEM)
params = pltpu.CompilerParams(vmem_limit_bytes=vmem_bytes)


def pack_kernel(cuts, capacity, place_ref, rows_ref, grad_ref, *refs):
    outs, (columns_ref, sems) = refs[:6], refs[6:]
    flat_count = grad_ref.shape[1]
    copies = []
    for g in range(3):
        part = pl.ds(cuts[g], cuts[g + 1] - cuts[g])
        copies.append(pltpu.make_async_copy(grad_ref.at[0, :, part], columns_ref.at[:, part], sems.at[g]))
        copies[-1].start()
    half = 4 * capacity
    for g in range(3):
        hot = slots_to_rows(rows_ref, place_ref[0], place_ref[1], orders[g], capacity, flat_count)
        hot = hot.astype(jnp.bfloat16)
        copies[g].wait()
        columns = columns_ref[:, cuts[g] : cuts[g + 1]].astype(jnp.bfloat16)
        packed = jnp.dot(hot, columns, preferred_element_type=jnp.float32).astype(jnp.bfloat16)
        outs[g][...] = packed[half:]
        outs[3 + g][...] = packed[:half]


def pack(where, rows_by_shard, gradients, cuts, capacity):
    flat_count, width = gradients.shape[1:]
    shapes = [
        jax.ShapeDtypeStruct((4 * capacity, cuts[g + 1] - cuts[g]), jnp.bfloat16) for g in (0, 1, 2, 0, 1, 2)
    ]
    return pl.pallas_call(
        lambda *refs: pack_kernel(cuts, capacity, *refs),
        in_specs=[smem_spec, smem_spec, pl.BlockSpec(memory_space=pltpu.HBM)],
        out_specs=[vmem_spec] * 6,
        out_shape=shapes,
        scratch_shapes=[pltpu.VMEM((flat_count, width), jnp.float32), pltpu.SemaphoreType.DMA((3,))],
        compiler_params=params,
        name="pack",
    )(where, rows_by_shard, gradients)


def sum_kernel(kept_ref, arrived_ref, sent_ref, next_ref):
    rest = next_ref.shape[0]
    sent_ref[...] = (
        kept_ref[rest:].astype(jnp.float32) + arrived_ref[rest:].astype(jnp.float32)
    ).astype(jnp.bfloat16)
    next_ref[...] = kept_ref[:rest].astype(jnp.float32) + arrived_ref[:rest].astype(jnp.float32)


def summed(kept, arrived):
    shape = (kept.shape[0] // 2, kept.shape[1])
    return pl.pallas_call(
        sum_kernel,
        in_specs=[vmem_spec] * 2,
        out_specs=[vmem_spec] * 2,
        out_shape=[jax.ShapeDtypeStruct(shape, jnp.bfloat16), jax.ShapeDtypeStruct(shape, jnp.float32)],
        compiler_params=params,
        name="sums",
    )(kept, arrived)


def join_kernel(here_ref, arrived_ref, out_ref):
    rows = here_ref.shape[0]
    out_ref[:rows] = here_ref[...]
    out_ref[rows:] = arrived_ref[...]


def joined(here, arrived):
    return pl.pallas_call(
        join_kernel,
        in_specs=[vmem_spec] * 2,
        out_specs=vmem_spec,
        out_shape=jax.ShapeDtypeStruct((2 * here.shape[0], here.shape[1]), jnp.bfloat16),
        compiler_params=params,
        name="join",
    )(here, arrived)


def finish_kernel(cuts, capacity, place_ref, rows_ref, *refs):
    here, arrived, moved, own = refs[:3], refs[3:6], refs[6:8], refs[8:10]
    placed_ref, moment_refs = refs[10], refs[11:13]
    rows_out, moments_out, sems = refs[13:]
    moves = place_ref[2] != place_ref[0]
    copies = []
    for m in range(2):
        moments_out[m] = jnp.where(moves, moved[m][...].astype(jnp.float32), own[m][...])
        copies.append(pltpu.make_async_copy(moments_out.at[m], moment_refs[m].at[0], sems.at[m]))
        copies[-1].start()
    for g in range(3):
        part = pl.ds(cuts[g], cuts[g + 1] - cuts[g])
        hot = slots_to_rows(rows_ref, place_ref[2], place_ref[1], orders[g], capacity, rows_out.shape[0])
        hot = hot.T.astype(jnp.bfloat16)
        rows = jnp.concatenate([here[g][...], arrived[g][...]], axis=0)
        total = jnp.dot(hot, rows, preferred_element_type=jnp.float32)
        rows_out[:, cuts[g] : cuts[g + 1]] = total.astype(jnp.bfloat16)
        copies.append(pltpu.make_async_copy(rows_out.at[:, part], placed_ref.at[:, part], sems.at[2 + g]))
        copies[-1].start()
    for copy in copies:
        copy.wait()


def finished(where, rows_by_shard, here, arrived, moved, own, cuts, flat_count):
    capacity, width = own[0].shape
    hbm_spec = pl.BlockSpec(memory_space=pltpu.HBM)
    moment = jax.ShapeDtypeStruct((1, capacity, width), jnp.float32)
    return pl.pallas_call(
        lambda *refs: finish_kernel(cuts, capacity, *refs),
        in_specs=[smem_spec, smem_spec] + [vmem_spec] * 10,
        out_specs=[hbm_spec] * 3,
        out_shape=[jax.ShapeDtypeStruct((flat_count, width), jnp.bfloat16), moment, moment],
        scratch_shapes=[
            pltpu.VMEM((flat_count, width), jnp.bfloat16),
            pltpu.VMEM((2, capacity, width), jnp.float32),
            pltpu.SemaphoreType.DMA((5,)),
        ],
        compiler_params=params,
        name="finish",
    )(where, rows_by_shard, *here, *arrived, *moved, *own)


def body(gradients, master_rows, first_moment, second_moment, shard_rows, move_partner):
    capacity = master_rows.shape[1]
    flat_count, width = gradients.shape[1:]
    lanes = width // 128
    cuts = [128 * (lanes * i // 3) for i in range(4)]
    dp_index = lax.axis_index("dp")
    ep_index = lax.axis_index("ep")
    ep_all = jnp.arange(move_partner.shape[0], dtype=jnp.int32)
    where = jnp.stack([ep_index, dp_index]).astype(jnp.int32)

    rows_by_shard = shard_rows.T
    packed = pack(where, rows_by_shard, gradients, cuts, capacity)
    grads = []
    for g, order in enumerate(orders):
        sent, kept = packed[g], packed[3 + g]
        for step in range(3):
            arrived = flipped_by(sent, "dp", order[step])
            if step < 2:
                sent, kept = summed(kept, arrived)
        grads.append(kept + arrived.astype(jnp.float32))
    grad_own = jnp.concatenate(grads, axis=1) / 8

    partner = jnp.sum(jnp.where(ep_all == ep_index, move_partner, 0))
    own_counts = jnp.sum(jnp.where((ep_all == ep_index)[:, None], shard_rows, 0), axis=0)
    own_count = jnp.sum(jnp.where(jnp.arange(8, dtype=jnp.int32) == dp_index, own_counts, 0))
    live = (jnp.arange(capacity, dtype=jnp.int32) < own_count)[:, None]
    moves = partner != ep_index
    flips = jnp.bitwise_xor(move_partner, ep_all)
    bits = move_partner.shape[0].bit_length() - 1
    which_bit = jnp.max(sum((flips >= 1 << b).astype(jnp.int32) for b in range(1, bits)))

    sent_master = adam_step(grad_own, master_rows[0], first_moment[0], second_moment[0], live)[0]
    sent_master = sent_master.astype(jnp.bfloat16)
    (there,) = lax.switch(
        which_bit,
        [lambda o, b=b: [flipped_by(a, "ep", 1 << b) for a in o] for b in range(bits)],
        [sent_master],
    )
    narrow = jnp.where(moves, there, sent_master)
    here = [narrow[:, cuts[g] : cuts[g + 1]] for g in range(3)]
    here = [joined(h, flipped_by(h, "dp", order[2])) for h, order in zip(here, orders)]
    here, grad_own = lax.optimization_barrier((here, grad_own))
    updated, first_new, second_new = adam_step(
        grad_own, master_rows[0], first_moment[0], second_moment[0], live
    )
    here = [joined(h, flipped_by(h, "dp", order[1])) for h, order in zip(here, orders)]

    def last(apart, operands):
        here, moments = operands
        arrived = [flipped_by(here[g], "dp", orders[g][0]) for g in range(3)]
        return arrived, [flipped_by(m, "ep", 1 << apart) for m in moments]

    moments = [first_new.astype(jnp.bfloat16), second_new.astype(jnp.bfloat16)]
    arrived, moments = lax.switch(
        which_bit, [lambda o, b=b: last(b, o) for b in range(bits)], (here, moments)
    )
    placed, new_first, new_second = finished(
        jnp.stack([ep_index, dp_index, partner]).astype(jnp.int32),
        rows_by_shard,
        here,
        arrived,
        moments,
        (first_new, second_new),
        cuts,
        flat_count,
    )
    new_master = jnp.where(moves, narrow.astype(jnp.float32), updated)[None]
    return new_master, new_first, new_second, placed


def solution(mesh):
    placed = (
        P("dp", "ep", None),
        P("ep", "dp", None),
        P("ep", "dp", None),
        P("ep", "dp", None),
        P(),
        P(),
    )
    return jax.shard_map(
        body,
        mesh=mesh,
        in_specs=placed,
        out_specs=(P("ep", "dp", None), P("ep", "dp", None), P("ep", "dp", None), P("ep", None)),
        check_vma=False,
    )
```

```python
import jax
import jax.numpy as jnp
from jax import lax
from jax.experimental import pallas as pl
from jax.experimental.pallas import tpu as pltpu
from jax.sharding import PartitionSpec as P

beta_one = 0.9
beta_two = 0.95
learn_rate = 0.02
weight_decay = 0.1
epsilon = 1e-08
correct_one = 1.0 - 0.9**10
correct_two = 1.0 - 0.95**10

orders = ((4, 1, 3), (1, 3, 4), (3, 4, 1))
mebibyte = 1024 * 1024


def flipped_by(array, axis, mask):
    return lax.ppermute(array, axis, [(i, i ^ mask) for i in range(lax.axis_size(axis))])


def adam_step(grad_rows, weights, first, second, live):
    first_new = beta_one * first + (1.0 - beta_one) * grad_rows
    second_new = beta_two * second + (1.0 - beta_two) * grad_rows * grad_rows
    ratio = first_new / correct_one / (jnp.sqrt(second_new / correct_two) + epsilon)
    updated = weights - learn_rate * (ratio + weight_decay * weights)
    return (
        jnp.where(live, updated, 0.0),
        jnp.where(live, first_new, 0.0),
        jnp.where(live, second_new, 0.0),
    )


def slots_to_rows(rows_ref, ep_index, dp_index, order, capacity, flat_count):
    shards = rows_ref.shape[0]
    counts = [rows_ref[k, ep_index] for k in range(shards)]
    starts = [jnp.int32(0)]
    for k in range(shards - 1):
        starts.append(starts[-1] + counts[k])
    slot = lax.broadcasted_iota(jnp.int32, (capacity, flat_count), 0)
    flat = lax.broadcasted_iota(jnp.int32, (capacity, flat_count), 1)
    blocks = []
    for p in range(shards):
        k = dp_index ^ ((p >> 2 & 1) * order[0] ^ (p >> 1 & 1) * order[1] ^ (p & 1) * order[2])
        start, count = starts[0], counts[0]
        for j in range(1, shards):
            start = jnp.where(k == j, starts[j], start)
            count = jnp.where(k == j, counts[j], count)
        blocks.append(jnp.where((flat - slot == start) & (slot < count), 1.0, 0.0))
    return jnp.concatenate(blocks, axis=0)


smem_spec = pl.BlockSpec(memory_space=pltpu.SMEM)
vmem_spec = pl.BlockSpec(memory_space=pltpu.VMEM)


def params(mebibytes):
    return pltpu.CompilerParams(vmem_limit_bytes=mebibytes * mebibyte)


def pack_kernel(cuts, capacity, place_ref, rows_ref, grad_ref, *refs):
    outs, (columns_ref, sems) = refs[:6], refs[6:]
    flat_count = grad_ref.shape[1]
    copies = []
    for g in range(3):
        part = pl.ds(cuts[g], cuts[g + 1] - cuts[g])
        copies.append(pltpu.make_async_copy(grad_ref.at[0, :, part], columns_ref.at[:, part], sems.at[g]))
        copies[-1].start()
    half = 4 * capacity
    for g in range(3):
        hot = slots_to_rows(rows_ref, place_ref[0], place_ref[1], orders[g], capacity, flat_count)
        hot = hot.astype(jnp.bfloat16)
        copies[g].wait()
        columns = columns_ref[:, cuts[g] : cuts[g + 1]].astype(jnp.bfloat16)
        packed = jnp.dot(hot, columns, preferred_element_type=jnp.float32).astype(jnp.bfloat16)
        outs[g][...] = packed[half:]
        outs[3 + g][...] = packed[:half]


def pack(where, rows_by_shard, gradients, cuts, capacity):
    flat_count, width = gradients.shape[1:]
    shapes = [
        jax.ShapeDtypeStruct((4 * capacity, cuts[g + 1] - cuts[g]), jnp.bfloat16) for g in (0, 1, 2, 0, 1, 2)
    ]
    return pl.pallas_call(
        lambda *refs: pack_kernel(cuts, capacity, *refs),
        in_specs=[smem_spec, smem_spec, pl.BlockSpec(memory_space=pltpu.HBM)],
        out_specs=[vmem_spec] * 6,
        out_shape=shapes,
        scratch_shapes=[pltpu.VMEM((flat_count, width), jnp.float32), pltpu.SemaphoreType.DMA((3,))],
        compiler_params=params(48),
        name="pack",
    )(where, rows_by_shard, gradients)


def sum_kernel(kept_ref, arrived_ref, sent_ref, next_ref):
    rest = next_ref.shape[0]
    sent_ref[...] = (
        kept_ref[rest:].astype(jnp.float32) + arrived_ref[rest:].astype(jnp.float32)
    ).astype(jnp.bfloat16)
    next_ref[...] = kept_ref[:rest].astype(jnp.float32) + arrived_ref[:rest].astype(jnp.float32)


def summed(kept, arrived):
    shape = (kept.shape[0] // 2, kept.shape[1])
    return pl.pallas_call(
        sum_kernel,
        in_specs=[vmem_spec] * 2,
        out_specs=[vmem_spec] * 2,
        out_shape=[jax.ShapeDtypeStruct(shape, jnp.bfloat16), jax.ShapeDtypeStruct(shape, jnp.float32)],
        compiler_params=params(6),
        name="sums",
    )(kept, arrived)


def join_kernel(*refs):
    count = len(refs) // 3
    for here_ref, arrived_ref, out_ref in zip(refs[:count], refs[count : 2 * count], refs[2 * count :]):
        rows = here_ref.shape[0]
        out_ref[:rows] = here_ref[...]
        out_ref[rows:] = arrived_ref[...]


def joined(here, arrived):
    return pl.pallas_call(
        join_kernel,
        in_specs=[vmem_spec] * (2 * len(here)),
        out_specs=[vmem_spec] * len(here),
        out_shape=[jax.ShapeDtypeStruct((2 * h.shape[0], h.shape[1]), jnp.bfloat16) for h in here],
        compiler_params=params(6),
        name="join",
    )(*here, *arrived)


def finish_kernel(cuts, capacity, place_ref, rows_ref, *refs):
    here, arrived, moved, own = refs[:3], refs[3:6], refs[6:8], refs[8:10]
    placed_ref, moment_refs = refs[10], refs[11:13]
    rows_out, moments_out, sems = refs[13:]
    moves = place_ref[2] != place_ref[0]
    copies = []
    for m in range(2):
        moments_out[m] = jnp.where(moves, moved[m][...].astype(jnp.float32), own[m][...])
        copies.append(pltpu.make_async_copy(moments_out.at[m], moment_refs[m].at[0], sems.at[m]))
        copies[-1].start()
    for g in range(3):
        part = pl.ds(cuts[g], cuts[g + 1] - cuts[g])
        hot = slots_to_rows(rows_ref, place_ref[2], place_ref[1], orders[g], capacity, rows_out.shape[0])
        hot = hot.T.astype(jnp.bfloat16)
        rows = jnp.concatenate([here[g][...], arrived[g][...]], axis=0)
        total = jnp.dot(hot, rows, preferred_element_type=jnp.float32)
        rows_out[:, cuts[g] : cuts[g + 1]] = total.astype(jnp.bfloat16)
        copies.append(pltpu.make_async_copy(rows_out.at[:, part], placed_ref.at[:, part], sems.at[2 + g]))
        copies[-1].start()
    for copy in copies:
        copy.wait()


def finished(where, rows_by_shard, here, arrived, moved, own, cuts, flat_count):
    capacity, width = own[0].shape
    hbm_spec = pl.BlockSpec(memory_space=pltpu.HBM)
    moment = jax.ShapeDtypeStruct((1, capacity, width), jnp.float32)
    return pl.pallas_call(
        lambda *refs: finish_kernel(cuts, capacity, *refs),
        in_specs=[smem_spec, smem_spec] + [vmem_spec] * 10,
        out_specs=[hbm_spec] * 3,
        out_shape=[jax.ShapeDtypeStruct((flat_count, width), jnp.bfloat16), moment, moment],
        scratch_shapes=[
            pltpu.VMEM((flat_count, width), jnp.bfloat16),
            pltpu.VMEM((2, capacity, width), jnp.float32),
            pltpu.SemaphoreType.DMA((5,)),
        ],
        compiler_params=params(18),
        name="finish",
    )(where, rows_by_shard, *here, *arrived, *moved, *own)


def body(gradients, master_rows, first_moment, second_moment, shard_rows, move_partner):
    capacity = master_rows.shape[1]
    flat_count, width = gradients.shape[1:]
    lanes = width // 128
    cuts = [128 * (lanes * i // 3) for i in range(4)]
    dp_index = lax.axis_index("dp")
    ep_index = lax.axis_index("ep")
    ep_all = jnp.arange(move_partner.shape[0], dtype=jnp.int32)
    where = jnp.stack([ep_index, dp_index]).astype(jnp.int32)

    rows_by_shard = shard_rows.T
    packed = pack(where, rows_by_shard, gradients, cuts, capacity)
    first_sent, first_kept = packed[:3], list(packed[3:])
    partner = jnp.sum(jnp.where(ep_all == ep_index, move_partner, 0))
    own_counts = jnp.sum(jnp.where((ep_all == ep_index)[:, None], shard_rows, 0), axis=0)
    own_count = jnp.sum(jnp.where(jnp.arange(8, dtype=jnp.int32) == dp_index, own_counts, 0))
    flips = jnp.bitwise_xor(move_partner, ep_all)
    bits = move_partner.shape[0].bit_length() - 1
    which_bit = jnp.max(sum((flips >= 1 << b).astype(jnp.int32) for b in range(1, bits)))
    moved_where = jnp.stack([ep_index, dp_index, partner]).astype(jnp.int32)
    first_kept[0], own_count, moved_where, which_bit = lax.optimization_barrier(
        (first_kept[0], own_count, moved_where, which_bit)
    )
    live = (jnp.arange(capacity, dtype=jnp.int32) < own_count)[:, None]
    moves = moved_where[2] != ep_index
    grads = []
    for g, order in enumerate(orders):
        sent, kept = first_sent[g], first_kept[g]
        for step in range(3):
            arrived = flipped_by(sent, "dp", order[step])
            if step < 2:
                sent, kept = summed(kept, arrived)
        grads.append(kept + arrived.astype(jnp.float32))
    grad_own = jnp.concatenate(grads, axis=1) / 8

    updated, first_new, second_new = adam_step(
        grad_own, master_rows[0], first_moment[0], second_moment[0], live
    )
    sent_master = updated.astype(jnp.bfloat16)
    (there,) = lax.switch(
        which_bit,
        [lambda o, b=b: [flipped_by(a, "ep", 1 << b) for a in o] for b in range(bits)],
        [sent_master],
    )
    narrow = jnp.where(moves, there, sent_master)
    here = [narrow[:, cuts[g] : cuts[g + 1]] for g in range(3)]
    for step in (2, 1):
        here = [joined([h], [flipped_by(h, "dp", order[step])])[0] for h, order in zip(here, orders)]

    def last(apart, operands):
        here, moments = operands
        arrived = [flipped_by(h, "dp", order[0]) for h, order in zip(here, orders)]
        return arrived, [flipped_by(m, "ep", 1 << apart) for m in moments]

    moments = [first_new.astype(jnp.bfloat16), second_new.astype(jnp.bfloat16)]
    arrived, moments = lax.switch(
        which_bit, [lambda o, b=b: last(b, o) for b in range(bits)], (here, moments)
    )
    placed, new_first, new_second = finished(
        moved_where,
        rows_by_shard,
        here,
        arrived,
        moments,
        (first_new, second_new),
        cuts,
        flat_count,
    )
    new_master = jnp.where(moves, narrow.astype(jnp.float32), updated)[None]
    return new_master, new_first, new_second, placed


def solution(mesh):
    placed = (
        P("dp", "ep", None),
        P("ep", "dp", None),
        P("ep", "dp", None),
        P("ep", "dp", None),
        P(),
        P(),
    )
    return jax.shard_map(
        body,
        mesh=mesh,
        in_specs=placed,
        out_specs=(P("ep", "dp", None), P("ep", "dp", None), P("ep", "dp", None), P("ep", None)),
        check_vma=False,
    )
```

```python
import jax
import jax.numpy as jnp
from jax import lax
from jax.experimental import pallas as pl
from jax.experimental.pallas import tpu as pltpu
from jax.sharding import PartitionSpec as P

beta_one = 0.9
beta_two = 0.95
learn_rate = 0.02
weight_decay = 0.1
epsilon = 1e-08
correct_one = 1.0 - 0.9**10
correct_two = 1.0 - 0.95**10

orders = ((4, 1, 3), (1, 3, 4), (3, 4, 1))
mebibyte = 1024 * 1024


def flipped_by(array, axis, mask):
    return lax.ppermute(array, axis, [(i, i ^ mask) for i in range(lax.axis_size(axis))])


def adam_step(grad_rows, weights, first, second, live):
    first_new = beta_one * first + (1.0 - beta_one) * grad_rows
    second_new = beta_two * second + (1.0 - beta_two) * grad_rows * grad_rows
    ratio = first_new / correct_one / (jnp.sqrt(second_new / correct_two) + epsilon)
    updated = weights - learn_rate * (ratio + weight_decay * weights)
    return (
        jnp.where(live, updated, 0.0),
        jnp.where(live, first_new, 0.0),
        jnp.where(live, second_new, 0.0),
    )


def slots_to_rows(rows_ref, ep_index, dp_index, order, capacity, flat_count):
    shards = rows_ref.shape[0]
    counts = [rows_ref[k, ep_index] for k in range(shards)]
    starts = [jnp.int32(0)]
    for k in range(shards - 1):
        starts.append(starts[-1] + counts[k])
    slot = lax.broadcasted_iota(jnp.int32, (capacity, flat_count), 0)
    flat = lax.broadcasted_iota(jnp.int32, (capacity, flat_count), 1)
    blocks = []
    for p in range(shards):
        k = dp_index ^ ((p >> 2 & 1) * order[0] ^ (p >> 1 & 1) * order[1] ^ (p & 1) * order[2])
        start, count = starts[0], counts[0]
        for j in range(1, shards):
            start = jnp.where(k == j, starts[j], start)
            count = jnp.where(k == j, counts[j], count)
        blocks.append(jnp.where((flat - slot == start) & (slot < count), 1.0, 0.0))
    return jnp.concatenate(blocks, axis=0)


smem_spec = pl.BlockSpec(memory_space=pltpu.SMEM)
vmem_spec = pl.BlockSpec(memory_space=pltpu.VMEM)


def params(mebibytes):
    return pltpu.CompilerParams(vmem_limit_bytes=mebibytes * mebibyte)


def pack_kernel(cuts, capacity, place_ref, rows_ref, grad_ref, *refs):
    outs, (columns_ref, sems) = refs[:6], refs[6:]
    flat_count = grad_ref.shape[1]
    copies = []
    for g in range(3):
        part = pl.ds(cuts[g], cuts[g + 1] - cuts[g])
        copies.append(pltpu.make_async_copy(grad_ref.at[0, :, part], columns_ref.at[:, part], sems.at[g]))
        copies[-1].start()
    half = 4 * capacity
    for g in range(3):
        hot = slots_to_rows(rows_ref, place_ref[0], place_ref[1], orders[g], capacity, flat_count)
        hot = hot.astype(jnp.bfloat16)
        copies[g].wait()
        columns = columns_ref[:, cuts[g] : cuts[g + 1]].astype(jnp.bfloat16)
        packed = jnp.dot(hot, columns, preferred_element_type=jnp.float32).astype(jnp.bfloat16)
        outs[g][...] = packed[half:]
        outs[3 + g][...] = packed[:half]


def pack(where, rows_by_shard, gradients, cuts, capacity):
    flat_count, width = gradients.shape[1:]
    shapes = [
        jax.ShapeDtypeStruct((4 * capacity, cuts[g + 1] - cuts[g]), jnp.bfloat16) for g in (0, 1, 2, 0, 1, 2)
    ]
    return pl.pallas_call(
        lambda *refs: pack_kernel(cuts, capacity, *refs),
        in_specs=[smem_spec, smem_spec, pl.BlockSpec(memory_space=pltpu.HBM)],
        out_specs=[vmem_spec] * 6,
        out_shape=shapes,
        scratch_shapes=[pltpu.VMEM((flat_count, width), jnp.float32), pltpu.SemaphoreType.DMA((3,))],
        compiler_params=params(48),
        name="pack",
    )(where, rows_by_shard, gradients)


def sum_kernel(kept_ref, arrived_ref, sent_ref, next_ref):
    rest = next_ref.shape[0]
    sent_ref[...] = (
        kept_ref[rest:].astype(jnp.float32) + arrived_ref[rest:].astype(jnp.float32)
    ).astype(jnp.bfloat16)
    next_ref[...] = kept_ref[:rest].astype(jnp.float32) + arrived_ref[:rest].astype(jnp.float32)


def summed(kept, arrived):
    shape = (kept.shape[0] // 2, kept.shape[1])
    return pl.pallas_call(
        sum_kernel,
        in_specs=[vmem_spec] * 2,
        out_specs=[vmem_spec] * 2,
        out_shape=[jax.ShapeDtypeStruct(shape, jnp.bfloat16), jax.ShapeDtypeStruct(shape, jnp.float32)],
        compiler_params=params(6),
        name="sums",
    )(kept, arrived)


def join_kernel(*refs):
    count = len(refs) // 3
    for here_ref, arrived_ref, out_ref in zip(refs[:count], refs[count : 2 * count], refs[2 * count :]):
        rows = here_ref.shape[0]
        out_ref[:rows] = here_ref[...]
        out_ref[rows:] = arrived_ref[...]


def joined(here, arrived):
    return pl.pallas_call(
        join_kernel,
        in_specs=[vmem_spec] * (2 * len(here)),
        out_specs=[vmem_spec] * len(here),
        out_shape=[jax.ShapeDtypeStruct((2 * h.shape[0], h.shape[1]), jnp.bfloat16) for h in here],
        compiler_params=params(6),
        name="join",
    )(*here, *arrived)


def finish_kernel(cuts, capacity, place_ref, rows_ref, *refs):
    here, arrived, moved, own = refs[:3], refs[3:6], refs[6:8], refs[8:10]
    placed_ref, moment_refs = refs[10], refs[11:13]
    rows_out, moments_out, sems = refs[13:]
    moves = place_ref[2] != place_ref[0]
    copies = []
    for m in range(2):
        moments_out[m] = jnp.where(moves, moved[m][...].astype(jnp.float32), own[m][...])
        copies.append(pltpu.make_async_copy(moments_out.at[m], moment_refs[m].at[0], sems.at[m]))
        copies[-1].start()
    for g in range(3):
        part = pl.ds(cuts[g], cuts[g + 1] - cuts[g])
        hot = slots_to_rows(rows_ref, place_ref[2], place_ref[1], orders[g], capacity, rows_out.shape[0])
        hot = hot.T.astype(jnp.bfloat16)
        rows = jnp.concatenate([here[g][...], arrived[g][...]], axis=0)
        total = jnp.dot(hot, rows, preferred_element_type=jnp.float32)
        rows_out[:, cuts[g] : cuts[g + 1]] = total.astype(jnp.bfloat16)
        copies.append(pltpu.make_async_copy(rows_out.at[:, part], placed_ref.at[:, part], sems.at[2 + g]))
        copies[-1].start()
    for copy in copies:
        copy.wait()


def finished(where, rows_by_shard, here, arrived, moved, own, cuts, flat_count):
    capacity, width = own[0].shape
    hbm_spec = pl.BlockSpec(memory_space=pltpu.HBM)
    moment = jax.ShapeDtypeStruct((1, capacity, width), jnp.float32)
    return pl.pallas_call(
        lambda *refs: finish_kernel(cuts, capacity, *refs),
        in_specs=[smem_spec, smem_spec] + [vmem_spec] * 10,
        out_specs=[hbm_spec] * 3,
        out_shape=[jax.ShapeDtypeStruct((flat_count, width), jnp.bfloat16), moment, moment],
        scratch_shapes=[
            pltpu.VMEM((flat_count, width), jnp.bfloat16),
            pltpu.VMEM((2, capacity, width), jnp.float32),
            pltpu.SemaphoreType.DMA((5,)),
        ],
        compiler_params=params(18),
        name="finish",
    )(where, rows_by_shard, *here, *arrived, *moved, *own)


def body(gradients, master_rows, first_moment, second_moment, shard_rows, move_partner):
    capacity = master_rows.shape[1]
    flat_count, width = gradients.shape[1:]
    lanes = width // 128
    cuts = [128 * (lanes * i // 3) for i in range(4)]
    dp_index = lax.axis_index("dp")
    ep_index = lax.axis_index("ep")
    ep_all = jnp.arange(move_partner.shape[0], dtype=jnp.int32)
    where = jnp.stack([ep_index, dp_index]).astype(jnp.int32)

    rows_by_shard = shard_rows.T
    packed = pack(where, rows_by_shard, gradients, cuts, capacity)
    first_sent, first_kept = packed[:3], list(packed[3:])
    partner = jnp.sum(jnp.where(ep_all == ep_index, move_partner, 0))
    own_counts = jnp.sum(jnp.where((ep_all == ep_index)[:, None], shard_rows, 0), axis=0)
    own_count = jnp.sum(jnp.where(jnp.arange(8, dtype=jnp.int32) == dp_index, own_counts, 0))
    flips = jnp.bitwise_xor(move_partner, ep_all)
    bits = move_partner.shape[0].bit_length() - 1
    which_bit = jnp.max(sum((flips >= 1 << b).astype(jnp.int32) for b in range(1, bits)))
    moved_where = jnp.stack([ep_index, dp_index, partner]).astype(jnp.int32)
    first_kept[0], own_count, moved_where, which_bit = lax.optimization_barrier(
        (first_kept[0], own_count, moved_where, which_bit)
    )
    live = (jnp.arange(capacity, dtype=jnp.int32) < own_count)[:, None]
    moves = moved_where[2] != ep_index
    grads = []
    for g, order in enumerate(orders):
        sent, kept = first_sent[g], first_kept[g]
        for step in range(3):
            arrived = flipped_by(sent, "dp", order[step])
            if step < 2:
                sent, kept = summed(kept, arrived)
        grads.append(kept + arrived.astype(jnp.float32))
    grad_own = lax.optimization_barrier(jnp.concatenate(grads, axis=1) / 8)

    sent_master = adam_step(grad_own, master_rows[0], first_moment[0], second_moment[0], live)[0]
    sent_master = sent_master.astype(jnp.bfloat16)
    (there,) = lax.switch(
        which_bit,
        [lambda o, b=b: [flipped_by(a, "ep", 1 << b) for a in o] for b in range(bits)],
        [sent_master],
    )
    narrow = jnp.where(moves, there, sent_master)
    here = [narrow[:, cuts[g] : cuts[g + 1]] for g in range(3)]
    here = [joined([h], [flipped_by(h, "dp", order[2])])[0] for h, order in zip(here, orders)]
    here, grad_own = lax.optimization_barrier((here, grad_own))
    updated, first_new, second_new = adam_step(
        grad_own, master_rows[0], first_moment[0], second_moment[0], live
    )
    here = [joined([h], [flipped_by(h, "dp", order[1])])[0] for h, order in zip(here, orders)]

    def last(apart, operands):
        here, moments = operands
        arrived = [flipped_by(h, "dp", order[0]) for h, order in zip(here, orders)]
        return arrived, [flipped_by(m, "ep", 1 << apart) for m in moments]

    moments = [first_new.astype(jnp.bfloat16), second_new.astype(jnp.bfloat16)]
    arrived, moments = lax.switch(
        which_bit, [lambda o, b=b: last(b, o) for b in range(bits)], (here, moments)
    )
    placed, new_first, new_second = finished(
        moved_where,
        rows_by_shard,
        here,
        arrived,
        moments,
        (first_new, second_new),
        cuts,
        flat_count,
    )
    new_master = jnp.where(moves, narrow.astype(jnp.float32), updated)[None]
    return new_master, new_first, new_second, placed


def solution(mesh):
    placed = (
        P("dp", "ep", None),
        P("ep", "dp", None),
        P("ep", "dp", None),
        P("ep", "dp", None),
        P(),
        P(),
    )
    return jax.shard_map(
        body,
        mesh=mesh,
        in_specs=placed,
        out_specs=(P("ep", "dp", None), P("ep", "dp", None), P("ep", "dp", None), P("ep", None)),
        check_vma=False,
    )
```

```python
import jax
import jax.numpy as jnp
from jax import lax
from jax.experimental import pallas as pl
from jax.experimental.pallas import tpu as pltpu
from jax.sharding import PartitionSpec as P

beta_one = 0.9
beta_two = 0.95
learn_rate = 0.02
weight_decay = 0.1
epsilon = 1e-08
correct_one = 1.0 - 0.9**10
correct_two = 1.0 - 0.95**10

orders = ((4, 1, 3), (1, 3, 4), (3, 4, 1))
mebibyte = 1024 * 1024


def flipped_by(array, axis, mask):
    return lax.ppermute(array, axis, [(i, i ^ mask) for i in range(lax.axis_size(axis))])


def adam_step(grad_rows, weights, first, second, live):
    first_new = beta_one * first + (1.0 - beta_one) * grad_rows
    second_new = beta_two * second + (1.0 - beta_two) * grad_rows * grad_rows
    ratio = first_new / correct_one / (jnp.sqrt(second_new / correct_two) + epsilon)
    updated = weights - learn_rate * (ratio + weight_decay * weights)
    return (
        jnp.where(live, updated, 0.0),
        jnp.where(live, first_new, 0.0),
        jnp.where(live, second_new, 0.0),
    )


def slots_to_rows(rows_ref, ep_index, dp_index, order, capacity, flat_count):
    shards = rows_ref.shape[0]
    counts = [rows_ref[k, ep_index] for k in range(shards)]
    starts = [jnp.int32(0)]
    for k in range(shards - 1):
        starts.append(starts[-1] + counts[k])
    slot = lax.broadcasted_iota(jnp.int32, (capacity, flat_count), 0)
    flat = lax.broadcasted_iota(jnp.int32, (capacity, flat_count), 1)
    blocks = []
    for p in range(shards):
        k = dp_index ^ ((p >> 2 & 1) * order[0] ^ (p >> 1 & 1) * order[1] ^ (p & 1) * order[2])
        start, count = starts[0], counts[0]
        for j in range(1, shards):
            start = jnp.where(k == j, starts[j], start)
            count = jnp.where(k == j, counts[j], count)
        blocks.append(jnp.where((flat - slot == start) & (slot < count), 1.0, 0.0))
    return jnp.concatenate(blocks, axis=0)


smem_spec = pl.BlockSpec(memory_space=pltpu.SMEM)
vmem_spec = pl.BlockSpec(memory_space=pltpu.VMEM)


def params(mebibytes):
    return pltpu.CompilerParams(vmem_limit_bytes=mebibytes * mebibyte)


def pack_kernel(cuts, capacity, place_ref, rows_ref, grad_ref, *refs):
    outs, (columns_ref, sems) = refs[:6], refs[6:]
    flat_count = grad_ref.shape[1]
    copies = []
    for g in range(3):
        part = pl.ds(cuts[g], cuts[g + 1] - cuts[g])
        copies.append(pltpu.make_async_copy(grad_ref.at[0, :, part], columns_ref.at[:, part], sems.at[g]))
        copies[-1].start()
    half = 4 * capacity
    for g in range(3):
        hot = slots_to_rows(rows_ref, place_ref[0], place_ref[1], orders[g], capacity, flat_count)
        hot = hot.astype(jnp.bfloat16)
        copies[g].wait()
        columns = columns_ref[:, cuts[g] : cuts[g + 1]].astype(jnp.bfloat16)
        packed = jnp.dot(hot, columns, preferred_element_type=jnp.float32).astype(jnp.bfloat16)
        outs[g][...] = packed[half:]
        outs[3 + g][...] = packed[:half]


def pack(where, rows_by_shard, gradients, cuts, capacity):
    flat_count, width = gradients.shape[1:]
    shapes = [
        jax.ShapeDtypeStruct((4 * capacity, cuts[g + 1] - cuts[g]), jnp.bfloat16) for g in (0, 1, 2, 0, 1, 2)
    ]
    return pl.pallas_call(
        lambda *refs: pack_kernel(cuts, capacity, *refs),
        in_specs=[smem_spec, smem_spec, pl.BlockSpec(memory_space=pltpu.HBM)],
        out_specs=[vmem_spec] * 6,
        out_shape=shapes,
        scratch_shapes=[pltpu.VMEM((flat_count, width), jnp.float32), pltpu.SemaphoreType.DMA((3,))],
        compiler_params=params(48),
        name="pack",
    )(where, rows_by_shard, gradients)


def sum_kernel(kept_ref, arrived_ref, sent_ref, next_ref):
    rest = next_ref.shape[0]
    sent_ref[...] = (
        kept_ref[rest:].astype(jnp.float32) + arrived_ref[rest:].astype(jnp.float32)
    ).astype(jnp.bfloat16)
    next_ref[...] = kept_ref[:rest].astype(jnp.float32) + arrived_ref[:rest].astype(jnp.float32)


def summed(kept, arrived):
    shape = (kept.shape[0] // 2, kept.shape[1])
    return pl.pallas_call(
        sum_kernel,
        in_specs=[vmem_spec] * 2,
        out_specs=[vmem_spec] * 2,
        out_shape=[jax.ShapeDtypeStruct(shape, jnp.bfloat16), jax.ShapeDtypeStruct(shape, jnp.float32)],
        compiler_params=params(6),
        name="sums",
    )(kept, arrived)


def join_kernel(*refs):
    count = len(refs) // 3
    for here_ref, arrived_ref, out_ref in zip(refs[:count], refs[count : 2 * count], refs[2 * count :]):
        rows = here_ref.shape[0]
        out_ref[:rows] = here_ref[...]
        out_ref[rows:] = arrived_ref[...]


def joined(here, arrived):
    return pl.pallas_call(
        join_kernel,
        in_specs=[vmem_spec] * (2 * len(here)),
        out_specs=[vmem_spec] * len(here),
        out_shape=[jax.ShapeDtypeStruct((2 * h.shape[0], h.shape[1]), jnp.bfloat16) for h in here],
        compiler_params=params(6),
        name="join",
    )(*here, *arrived)


def finish_kernel(cuts, capacity, place_ref, rows_ref, *refs):
    here, arrived, moved, own = refs[:3], refs[3:6], refs[6], refs[7:9]
    placed_ref, moment_refs = refs[9], refs[10:12]
    rows_out, moments_out, sems = refs[12:]
    moves = place_ref[2] != place_ref[0]
    copies = []
    for m in range(2):
        moments_out[m] = jnp.where(moves, moved[m].astype(jnp.float32), own[m][...])
        copies.append(pltpu.make_async_copy(moments_out.at[m], moment_refs[m].at[0], sems.at[m]))
        copies[-1].start()
    for g in range(3):
        part = pl.ds(cuts[g], cuts[g + 1] - cuts[g])
        hot = slots_to_rows(rows_ref, place_ref[2], place_ref[1], orders[g], capacity, rows_out.shape[0])
        hot = hot.T.astype(jnp.bfloat16)
        rows = jnp.concatenate([here[g][...], arrived[g][...]], axis=0)
        total = jnp.dot(hot, rows, preferred_element_type=jnp.float32)
        rows_out[:, cuts[g] : cuts[g + 1]] = total.astype(jnp.bfloat16)
        copies.append(pltpu.make_async_copy(rows_out.at[:, part], placed_ref.at[:, part], sems.at[2 + g]))
        copies[-1].start()
    for copy in copies:
        copy.wait()


def finished(where, rows_by_shard, here, arrived, moved, own, cuts, flat_count):
    capacity, width = own[0].shape
    hbm_spec = pl.BlockSpec(memory_space=pltpu.HBM)
    moment = jax.ShapeDtypeStruct((1, capacity, width), jnp.float32)
    return pl.pallas_call(
        lambda *refs: finish_kernel(cuts, capacity, *refs),
        in_specs=[smem_spec, smem_spec] + [vmem_spec] * 9,
        out_specs=[hbm_spec] * 3,
        out_shape=[jax.ShapeDtypeStruct((flat_count, width), jnp.bfloat16), moment, moment],
        scratch_shapes=[
            pltpu.VMEM((flat_count, width), jnp.bfloat16),
            pltpu.VMEM((2, capacity, width), jnp.float32),
            pltpu.SemaphoreType.DMA((5,)),
        ],
        compiler_params=params(18),
        name="finish",
    )(where, rows_by_shard, *here, *arrived, moved, *own)


def body(gradients, master_rows, first_moment, second_moment, shard_rows, move_partner):
    capacity = master_rows.shape[1]
    flat_count, width = gradients.shape[1:]
    lanes = width // 128
    cuts = [128 * (lanes * i // 3) for i in range(4)]
    dp_index = lax.axis_index("dp")
    ep_index = lax.axis_index("ep")
    ep_all = jnp.arange(move_partner.shape[0], dtype=jnp.int32)
    where = jnp.stack([ep_index, dp_index]).astype(jnp.int32)

    rows_by_shard = shard_rows.T
    packed = pack(where, rows_by_shard, gradients, cuts, capacity)
    first_sent, first_kept = packed[:3], list(packed[3:])
    partner = jnp.sum(jnp.where(ep_all == ep_index, move_partner, 0))
    own_counts = jnp.sum(jnp.where((ep_all == ep_index)[:, None], shard_rows, 0), axis=0)
    own_count = jnp.sum(jnp.where(jnp.arange(8, dtype=jnp.int32) == dp_index, own_counts, 0))
    flips = jnp.bitwise_xor(move_partner, ep_all)
    bits = move_partner.shape[0].bit_length() - 1
    which_bit = jnp.max(sum((flips >= 1 << b).astype(jnp.int32) for b in range(1, bits)))
    moved_where = jnp.stack([ep_index, dp_index, partner]).astype(jnp.int32)
    first_kept[0], own_count, moved_where, which_bit = lax.optimization_barrier(
        (first_kept[0], own_count, moved_where, which_bit)
    )
    live = (jnp.arange(capacity, dtype=jnp.int32) < own_count)[:, None]
    moves = moved_where[2] != ep_index
    grads = []
    for g, order in enumerate(orders):
        sent, kept = first_sent[g], first_kept[g]
        for step in range(3):
            arrived = flipped_by(sent, "dp", order[step])
            if step < 2:
                sent, kept = summed(kept, arrived)
        grads.append(kept + arrived.astype(jnp.float32))
    grad_own = lax.optimization_barrier(jnp.concatenate(grads, axis=1) / 8)

    sent_master = adam_step(grad_own, master_rows[0], first_moment[0], second_moment[0], live)[0]
    sent_master = sent_master.astype(jnp.bfloat16)
    (there,) = lax.switch(
        which_bit,
        [lambda o, b=b: [flipped_by(a, "ep", 1 << b) for a in o] for b in range(bits)],
        [sent_master],
    )
    narrow = jnp.where(moves, there, sent_master)
    here = [narrow[:, cuts[g] : cuts[g + 1]] for g in range(3)]
    here = [joined([h], [flipped_by(h, "dp", order[2])])[0] for h, order in zip(here, orders)]
    here, grad_own = lax.optimization_barrier((here, grad_own))
    updated, first_new, second_new = adam_step(
        grad_own, master_rows[0], first_moment[0], second_moment[0], live
    )
    here = [joined([h], [flipped_by(h, "dp", order[1])])[0] for h, order in zip(here, orders)]

    def last(apart, operands):
        here, moments = operands
        arrived = [flipped_by(h, "dp", order[0]) for h, order in zip(here, orders)]
        return arrived, flipped_by(moments, "ep", 1 << apart)

    moments = jnp.stack([first_new.astype(jnp.bfloat16), second_new.astype(jnp.bfloat16)])
    arrived, moments = lax.switch(
        which_bit, [lambda o, b=b: last(b, o) for b in range(bits)], (here, moments)
    )
    placed, new_first, new_second = finished(
        moved_where,
        rows_by_shard,
        here,
        arrived,
        moments,
        (first_new, second_new),
        cuts,
        flat_count,
    )
    new_master = jnp.where(moves, narrow.astype(jnp.float32), updated)[None]
    return new_master, new_first, new_second, placed


def solution(mesh):
    placed = (
        P("dp", "ep", None),
        P("ep", "dp", None),
        P("ep", "dp", None),
        P("ep", "dp", None),
        P(),
        P(),
    )
    return jax.shard_map(
        body,
        mesh=mesh,
        in_specs=placed,
        out_specs=(P("ep", "dp", None), P("ep", "dp", None), P("ep", "dp", None), P("ep", None)),
        check_vma=False,
    )
```

```python
import jax
import jax.numpy as jnp
from jax import lax
from jax.experimental import pallas as pl
from jax.experimental.pallas import tpu as pltpu
from jax.sharding import PartitionSpec as P

beta_one = 0.9
beta_two = 0.95
learn_rate = 0.02
weight_decay = 0.1
epsilon = 1e-08
correct_one = 1.0 - 0.9**10
correct_two = 1.0 - 0.95**10

orders = ((4, 1, 3), (1, 3, 4), (3, 4, 1))
mebibyte = 1024 * 1024


def flipped_by(array, axis, mask):
    return lax.ppermute(array, axis, [(i, i ^ mask) for i in range(lax.axis_size(axis))])


def adam_step(grad_rows, weights, first, second, live):
    first_new = beta_one * first + (1.0 - beta_one) * grad_rows
    second_new = beta_two * second + (1.0 - beta_two) * grad_rows * grad_rows
    ratio = first_new / correct_one / (jnp.sqrt(second_new / correct_two) + epsilon)
    updated = weights - learn_rate * (ratio + weight_decay * weights)
    return (
        jnp.where(live, updated, 0.0),
        jnp.where(live, first_new, 0.0),
        jnp.where(live, second_new, 0.0),
    )


def slots_to_rows(rows_ref, ep_index, dp_index, order, capacity, flat_count):
    shards = rows_ref.shape[0]
    counts = [rows_ref[k, ep_index] for k in range(shards)]
    starts = [jnp.int32(0)]
    for k in range(shards - 1):
        starts.append(starts[-1] + counts[k])
    slot = lax.broadcasted_iota(jnp.int32, (capacity, flat_count), 0)
    flat = lax.broadcasted_iota(jnp.int32, (capacity, flat_count), 1)
    blocks = []
    for p in range(shards):
        k = dp_index ^ ((p >> 2 & 1) * order[0] ^ (p >> 1 & 1) * order[1] ^ (p & 1) * order[2])
        start, count = starts[0], counts[0]
        for j in range(1, shards):
            start = jnp.where(k == j, starts[j], start)
            count = jnp.where(k == j, counts[j], count)
        blocks.append(jnp.where((flat - slot == start) & (slot < count), 1.0, 0.0))
    return jnp.concatenate(blocks, axis=0)


smem_spec = pl.BlockSpec(memory_space=pltpu.SMEM)
vmem_spec = pl.BlockSpec(memory_space=pltpu.VMEM)


def params(mebibytes):
    return pltpu.CompilerParams(vmem_limit_bytes=mebibytes * mebibyte)


def pack_kernel(cuts, capacity, place_ref, rows_ref, grad_ref, *refs):
    outs, (columns_ref, sems) = refs[:6], refs[6:]
    flat_count = grad_ref.shape[1]
    copies = []
    for g in range(3):
        part = pl.ds(cuts[g], cuts[g + 1] - cuts[g])
        copies.append(pltpu.make_async_copy(grad_ref.at[0, :, part], columns_ref.at[:, part], sems.at[g]))
        copies[-1].start()
    half = 4 * capacity
    for g in range(3):
        hot = slots_to_rows(rows_ref, place_ref[0], place_ref[1], orders[g], capacity, flat_count)
        hot = hot.astype(jnp.bfloat16)
        copies[g].wait()
        columns = columns_ref[:, cuts[g] : cuts[g + 1]].astype(jnp.bfloat16)
        packed = jnp.dot(hot, columns, preferred_element_type=jnp.float32).astype(jnp.bfloat16)
        outs[g][...] = packed[half:]
        outs[3 + g][...] = packed[:half]


def pack(where, rows_by_shard, gradients, cuts, capacity):
    flat_count, width = gradients.shape[1:]
    shapes = [
        jax.ShapeDtypeStruct((4 * capacity, cuts[g + 1] - cuts[g]), jnp.bfloat16) for g in (0, 1, 2, 0, 1, 2)
    ]
    return pl.pallas_call(
        lambda *refs: pack_kernel(cuts, capacity, *refs),
        in_specs=[smem_spec, smem_spec, pl.BlockSpec(memory_space=pltpu.HBM)],
        out_specs=[vmem_spec] * 6,
        out_shape=shapes,
        scratch_shapes=[pltpu.VMEM((flat_count, width), jnp.float32), pltpu.SemaphoreType.DMA((3,))],
        compiler_params=params(48),
        name="pack",
    )(where, rows_by_shard, gradients)


def sum_kernel(kept_ref, arrived_ref, sent_ref, next_ref):
    rest = next_ref.shape[0]
    sent_ref[...] = (
        kept_ref[rest:].astype(jnp.float32) + arrived_ref[rest:].astype(jnp.float32)
    ).astype(jnp.bfloat16)
    next_ref[...] = kept_ref[:rest].astype(jnp.float32) + arrived_ref[:rest].astype(jnp.float32)


def summed(kept, arrived):
    shape = (kept.shape[0] // 2, kept.shape[1])
    return pl.pallas_call(
        sum_kernel,
        in_specs=[vmem_spec] * 2,
        out_specs=[vmem_spec] * 2,
        out_shape=[jax.ShapeDtypeStruct(shape, jnp.bfloat16), jax.ShapeDtypeStruct(shape, jnp.float32)],
        compiler_params=params(6),
        name="sums",
    )(kept, arrived)


def join_kernel(*refs):
    count = len(refs) // 3
    for here_ref, arrived_ref, out_ref in zip(refs[:count], refs[count : 2 * count], refs[2 * count :]):
        rows = here_ref.shape[0]
        out_ref[:rows] = here_ref[...]
        out_ref[rows:] = arrived_ref[...]


def joined(here, arrived):
    return pl.pallas_call(
        join_kernel,
        in_specs=[vmem_spec] * (2 * len(here)),
        out_specs=[vmem_spec] * len(here),
        out_shape=[jax.ShapeDtypeStruct((2 * h.shape[0], h.shape[1]), jnp.bfloat16) for h in here],
        compiler_params=params(6),
        name="join",
    )(*here, *arrived)


def finish_kernel(cuts, capacity, place_ref, rows_ref, *refs):
    here, arrived, moved, own = refs[:3], refs[3:6], refs[6], refs[7:9]
    placed_ref, moment_refs = refs[9], refs[10:12]
    rows_out, moments_out, sems = refs[12:]
    moves = place_ref[2] != place_ref[0]
    copies = []
    for m in range(2):
        moments_out[m] = jnp.where(moves, moved[m].astype(jnp.float32), own[m][...])
        copies.append(pltpu.make_async_copy(moments_out.at[m], moment_refs[m].at[0], sems.at[m]))
        copies[-1].start()
    for g in range(3):
        part = pl.ds(cuts[g], cuts[g + 1] - cuts[g])
        hot = slots_to_rows(rows_ref, place_ref[2], place_ref[1], orders[g], capacity, rows_out.shape[0])
        hot = hot.T.astype(jnp.bfloat16)
        rows = jnp.concatenate([here[g][...], arrived[g][...]], axis=0)
        total = jnp.dot(hot, rows, preferred_element_type=jnp.float32)
        rows_out[:, cuts[g] : cuts[g + 1]] = total.astype(jnp.bfloat16)
        copies.append(pltpu.make_async_copy(rows_out.at[:, part], placed_ref.at[:, part], sems.at[2 + g]))
        copies[-1].start()
    for copy in copies:
        copy.wait()


def finished(where, rows_by_shard, here, arrived, moved, own, cuts, flat_count):
    capacity, width = own[0].shape
    hbm_spec = pl.BlockSpec(memory_space=pltpu.HBM)
    moment = jax.ShapeDtypeStruct((1, capacity, width), jnp.float32)
    return pl.pallas_call(
        lambda *refs: finish_kernel(cuts, capacity, *refs),
        in_specs=[smem_spec, smem_spec] + [vmem_spec] * 9,
        out_specs=[hbm_spec] * 3,
        out_shape=[jax.ShapeDtypeStruct((flat_count, width), jnp.bfloat16), moment, moment],
        scratch_shapes=[
            pltpu.VMEM((flat_count, width), jnp.bfloat16),
            pltpu.VMEM((2, capacity, width), jnp.float32),
            pltpu.SemaphoreType.DMA((5,)),
        ],
        compiler_params=params(18),
        name="finish",
    )(where, rows_by_shard, *here, *arrived, moved, *own)


def body(gradients, master_rows, first_moment, second_moment, shard_rows, move_partner):
    capacity = master_rows.shape[1]
    flat_count, width = gradients.shape[1:]
    lanes = width // 128
    cuts = [128 * (lanes * i // 3) for i in range(4)]
    dp_index = lax.axis_index("dp")
    ep_index = lax.axis_index("ep")
    ep_all = jnp.arange(move_partner.shape[0], dtype=jnp.int32)
    where = jnp.stack([ep_index, dp_index]).astype(jnp.int32)

    rows_by_shard = shard_rows.T
    packed = pack(where, rows_by_shard, gradients, cuts, capacity)
    first_sent, first_kept = packed[:3], list(packed[3:])
    partner = jnp.sum(jnp.where(ep_all == ep_index, move_partner, 0))
    own_counts = jnp.sum(jnp.where((ep_all == ep_index)[:, None], shard_rows, 0), axis=0)
    own_count = jnp.sum(jnp.where(jnp.arange(8, dtype=jnp.int32) == dp_index, own_counts, 0))
    flips = jnp.bitwise_xor(move_partner, ep_all)
    bits = move_partner.shape[0].bit_length() - 1
    which_bit = jnp.max(sum((flips >= 1 << b).astype(jnp.int32) for b in range(1, bits)))
    moved_where = jnp.stack([ep_index, dp_index, partner]).astype(jnp.int32)
    first_kept[0], own_count, moved_where, which_bit = lax.optimization_barrier(
        (first_kept[0], own_count, moved_where, which_bit)
    )
    live = (jnp.arange(capacity, dtype=jnp.int32) < own_count)[:, None]
    moves = moved_where[2] != ep_index
    grads = []
    for g, order in enumerate(orders):
        sent, kept = first_sent[g], first_kept[g]
        for step in range(3):
            arrived = flipped_by(sent, "dp", order[step])
            if step < 2:
                sent, kept = summed(kept, arrived)
        grads.append(kept + arrived.astype(jnp.float32))
    grad_own = lax.optimization_barrier(jnp.concatenate(grads, axis=1) / 8)

    sent_master = adam_step(grad_own, master_rows[0], first_moment[0], second_moment[0], live)[0]
    sent_master = sent_master.astype(jnp.bfloat16)
    (there,) = lax.switch(
        which_bit,
        [lambda o, b=b: [flipped_by(a, "ep", 1 << b) for a in o] for b in range(bits)],
        [sent_master],
    )
    narrow = jnp.where(moves, there, sent_master)
    here = [narrow[:, cuts[g] : cuts[g + 1]] for g in range(3)]
    here = [joined([h], [flipped_by(h, "dp", order[2])])[0] for h, order in zip(here, orders)]
    here, grad_own = lax.optimization_barrier((here, grad_own))
    updated, first_new, second_new = adam_step(
        grad_own, master_rows[0], first_moment[0], second_moment[0], live
    )
    here = [joined([h], [flipped_by(h, "dp", order[1])])[0] for h, order in zip(here, orders)]

    def last(apart, operands):
        here, moments = operands
        moved = flipped_by(moments, "ep", 1 << apart)
        arrived = [flipped_by(h, "dp", order[0]) for h, order in zip(here, orders)]
        return moved, arrived

    moments = jnp.stack([first_new.astype(jnp.bfloat16), second_new.astype(jnp.bfloat16)])
    moments, arrived = lax.switch(
        which_bit, [lambda o, b=b: last(b, o) for b in range(bits)], (here, moments)
    )
    placed, new_first, new_second = finished(
        moved_where,
        rows_by_shard,
        here,
        arrived,
        moments,
        (first_new, second_new),
        cuts,
        flat_count,
    )
    new_master = jnp.where(moves, narrow.astype(jnp.float32), updated)[None]
    return new_master, new_first, new_second, placed


def solution(mesh):
    placed = (
        P("dp", "ep", None),
        P("ep", "dp", None),
        P("ep", "dp", None),
        P("ep", "dp", None),
        P(),
        P(),
    )
    return jax.shard_map(
        body,
        mesh=mesh,
        in_specs=placed,
        out_specs=(P("ep", "dp", None), P("ep", "dp", None), P("ep", "dp", None), P("ep", None)),
        check_vma=False,
    )
```
